256 devices in a mesh: wide: 32 (over y, z), grp: 8 (over x, core).
Axes of the slice: x: 4, y: 4, z: 8, core: 2. Of those that a mesh axis runs over, the one named last changes fastest.
Arguments:
- tokens: bfloat16 [65536, 8192], P('wide', 'grp'), may hold values from -6 to 6
- value_weight: bfloat16 [8192, 1024], P('grp'), may hold values from -0.09375 to 0.09375
- down_panel_table: bfloat16 [1280, 64, 8192], P('wide', None, 'grp'), may hold values from -0.0625 to 0.0625
- up_panel_table: bfloat16 [1280, 64, 1024], P('wide', None, 'grp'), may hold values from -0.75 to 0.75
- request_adapter: int32 [32, 32], P('wide'), may hold values from 0 to 1279, as said below
- request_length: int32 [32, 32], P('wide'), may hold values from 1 to 128, 2048 in all within a row
- adapter_panel_place: int32 [1280], replicated, may hold values from 0 to 1279, as said below
Outputs:
- values_out: bfloat16 [65536, 1024], P('wide', 'grp')
The draws below stay inside these ranges and needn't reach their ends.
Inputs may be any that keep to these rules, and one draw needn't show every extreme that they name: `request_adapter`: each index of wide has at most 2 requests whose adapters share one owner; in every draw some owner receives exactly 2 from every index of wide. `request_length`: each row sums to 2048, and holds a request of exactly 128 rows. `adapter_panel_place`: A permutation of the adapters' panel slots.
All inputs are finite; a program needn't handle non-finite values.
Results may differ from the reference program's by a relative error of at most 0.0044.
Values may be sent and summed in bfloat16 or wider, within the bound.
A program may use at most 192 MiB of HBM per device.

```python
import math
import jax
import jax.numpy as jnp
import numpy as np
from jax import lax

MODEL_WIDTH = 8192
VALUE_UNITS = 1024
ADAPTER_RANK = 64
ADP_W = 40
BLOCK = 128
REQ_W = 32
OWNERS = 32
CAP_BLK = 2
TOKW = 2048
TOKENS = 65536
ADAPTER_TOTAL = 1280


def joint_routes(key):
    panel_slot = jax.random.permutation(jax.random.fold_in(key, 11), ADAPTER_TOTAL).astype(jnp.int32)
    inverse = jnp.argsort(panel_slot).astype(jnp.int32)
    popular = jax.random.randint(jax.random.fold_in(key, 12), (OWNERS,), 0, 4)
    hottest = jax.random.randint(jax.random.fold_in(key, 13), (), 0, OWNERS)
    candidate_count = OWNERS * CAP_BLK
    candidate = jnp.arange(candidate_count) // CAP_BLK
    device_keys = jax.random.split(jax.random.fold_in(key, 14), OWNERS)

    def pick(subkey):
        noise = jax.random.randint(subkey, (candidate_count,), 0, 1024)
        score = noise + popular[candidate] * 512 + (candidate == hottest).astype(jnp.int32) * 100000
        score = score * candidate_count + jnp.arange(candidate_count)
        ignored, chosen = lax.top_k(score, REQ_W)
        owner_index = candidate[chosen]
        shuffle = jax.random.permutation(jax.random.fold_in(subkey, 1), REQ_W)
        owner_index = owner_index[shuffle]
        local_index = jax.random.randint(jax.random.fold_in(subkey, 2), (REQ_W,), 0, ADP_W)
        return inverse[owner_index * ADP_W + local_index]
    adapters = jax.vmap(pick)(device_keys)
    return (panel_slot, adapters.astype(jnp.int32))


def draw_request_adapter(key, part):
    return joint_routes(key)[1]


def draw_adapter_panel_place(key, part):
    return joint_routes(key)[0]


def spiked(values, rng, source, target, parts, factor):
    owner, partner = [(jnp.arange(values.shape[dim]) // (values.shape[dim] // parts)).reshape([-1 if axis == dim else 1 for axis in range(values.ndim)]) for dim in (source, target)]
    chosen = jax.random.permutation(rng, parts)[partner]
    strong = (owner == chosen) | (owner == (partner + parts // 2) % parts)
    return jnp.where(strong, factor * values, values)


def level_of(rng, dims, cuts, least, high):
    factor_of = 1.0
    for axis_at, blocks in cuts:
        draws = jax.random.uniform(jax.random.fold_in(jax.random.fold_in(rng, 6), axis_at), (blocks,), jnp.float32, least / len(cuts), high / len(cuts))
        factor_of = factor_of * jnp.repeat(jnp.exp(draws), dims[axis_at] // blocks).reshape((-1,) + (1,) * (len(dims) - 1 - axis_at))
    return factor_of


def profile(count, total, bound, lean):
    loads = [(1 << 20) // math.isqrt(standing ** lean) + 1 for standing in range(2, count + 1)]
    surplus, holding = total - bound - (count - 1), [1] * (count - 1)
    while surplus > 0:
        candidates = [i for i in range(count - 1) if holding[i] < bound]
        whole, budget = sum([loads[i] for i in candidates]), surplus
        for i in candidates:
            more = min(bound - holding[i], max(1, budget * loads[i] // whole), surplus)
            holding[i] = holding[i] + more
            surplus = surplus - more
    return np.array([bound] + holding)


def uneven(rng, amount, total, limit, skew):
    if amount == 2:
        one = jax.random.randint(rng, (), max(1, total - limit), min(limit, total - 1) + 1)
        return jnp.stack([one, total - one])
    sizes = jnp.asarray(profile(amount, total, limit, skew), jnp.int32)
    pairs = (amount - 1) // 2
    source_of, receiver = sizes[1:1 + 2 * pairs:2], sizes[2:2 + 2 * pairs:2]
    margin = jnp.minimum(source_of - 1, limit - receiver)
    passed = jax.random.randint(jax.random.fold_in(rng, 1), (pairs,), 0, 1 << 20) % (margin + 1)
    sizes = sizes.at[1:1 + 2 * pairs:2].set(source_of - passed).at[2:2 + 2 * pairs:2].set(receiver + passed)
    return sizes[jax.random.permutation(jax.random.fold_in(rng, 2), amount)]


def scatter_about(stream_key, extent, width, reach, cuts=(), held_as=jnp.bfloat16):
    drawn = width * jax.random.normal(stream_key, extent, jnp.float32)
    if cuts:
        drawn = drawn * level_of(stream_key, extent, cuts, -0.22, 0.18)
    return jnp.clip(drawn, -reach, reach).astype(held_as)


def gaussian_with(rng, shape, deviation, bound, shards, heavy, held_as=jnp.bfloat16):
    result = deviation * jax.random.normal(rng, shape, jnp.float32)
    if shards:
        result = result * level_of(rng, shape, shards, -0.22, 0.18)
    return jnp.clip(spiked(result, jax.random.fold_in(rng, 3), *heavy), -bound, bound).astype(held_as)


def setup_inputs(seed: int = 0) -> dict:
    keys = jax.random.split(jax.random.key(seed), 8)
    return {
        "tokens": scatter_about(keys[0], (TOKENS, MODEL_WIDTH), 1.0, 6.0, ((0, 32), (1, 8))),
        "value_weight": gaussian_with(keys[1], (MODEL_WIDTH, VALUE_UNITS), MODEL_WIDTH ** -0.5, 0.09375, ((0, 8),), (0, 1, 8, 2.0)),
        "down_panel_table": scatter_about(keys[2], (ADAPTER_TOTAL, ADAPTER_RANK, MODEL_WIDTH), MODEL_WIDTH ** -0.5, 0.0625, ((0, 32), (2, 8))),
        "up_panel_table": scatter_about(keys[3], (ADAPTER_TOTAL, ADAPTER_RANK, VALUE_UNITS), ADAPTER_RANK ** -0.5, 0.75, ((0, 32), (2, 8))),
        "request_adapter": draw_request_adapter(jax.random.fold_in(keys[7], 71), 0),
        "request_length": jax.vmap(lambda own: uneven(own, REQ_W, TOKW, BLOCK, 2))(jax.random.split(keys[5], OWNERS)).reshape((OWNERS, REQ_W)).astype(jnp.int32),
        "adapter_panel_place": draw_adapter_panel_place(jax.random.fold_in(keys[7], 71), 0),
    }


def reference(tokens, value_weight, down_panel_table, up_panel_table, request_adapter, request_length, adapter_panel_place):
    base_sum = jnp.dot(tokens, value_weight, preferred_element_type=jnp.float32)
    offsets = jnp.arange(BLOCK)
    positions = jnp.arange(TOKW)
    request_ids = jnp.arange(REQ_W)

    def one_index(device_items):
        device_rows, adapters, lengths = device_items
        panel_positions = adapter_panel_place[adapters]
        starts = jnp.cumsum(lengths) - lengths
        row_index = starts[:, None] + offsets[None, :]
        within = offsets[None, :] < lengths[:, None]
        row_index = jnp.where(within, row_index, 0)
        token_blocks = jnp.where(within[:, :, None], device_rows[row_index], jnp.zeros((), device_rows.dtype))
        down_panels = down_panel_table[panel_positions].astype(jnp.float32)
        up_panels = up_panel_table[panel_positions].astype(jnp.float32)
        rank_projected = jnp.einsum('qbd,qrd->qbr', token_blocks.astype(jnp.float32), down_panels).astype(jnp.bfloat16)
        block_deltas = jnp.einsum('qbr,qre->qbe', rank_projected.astype(jnp.float32), up_panels).astype(jnp.bfloat16)
        ends = starts + lengths
        inside = (positions[:, None] >= starts[None, :]) & (positions[:, None] < ends[None, :])
        which_request = jnp.sum(jnp.where(inside, request_ids[None, :], 0), axis=1)
        offset = positions - jnp.sum(jnp.where(inside, starts[None, :], 0), axis=1)
        flat_delta = block_deltas.reshape(REQ_W * BLOCK, VALUE_UNITS)
        return flat_delta[which_request * BLOCK + offset]

    deltas = lax.map(one_index, (tokens.reshape(OWNERS, TOKW, MODEL_WIDTH), request_adapter, request_length))
    return (base_sum + deltas.reshape(TOKENS, VALUE_UNITS).astype(jnp.float32)).astype(jnp.bfloat16)
```

```python
import functools

import jax
import jax.numpy as jnp
from jax import lax
from jax.experimental import pallas as pl
from jax.experimental.pallas import tpu as pltpu
from jax.sharding import PartitionSpec as P

MESH = pl.DeviceIdType.MESH
ADP_W = 40
F32 = jnp.float32
BF16 = jnp.bfloat16
ROWS = 512


def routes(request_adapter, request_length, adapter_panel_place):
    adapters, lengths = request_adapter[0], request_length[0]
    count = adapters.shape[0]
    lookup = adapters[:, None] == jnp.arange(adapter_panel_place.shape[0])[None, :]
    panel_slot = jnp.sum(jnp.where(lookup, adapter_panel_place[None, :], 0), axis=1)
    owner = panel_slot // ADP_W
    local = panel_slot - owner * ADP_W
    before = jnp.arange(count)[None, :] < jnp.arange(count)[:, None]
    starts = jnp.sum(jnp.where(before, lengths[None, :], 0), axis=1)
    same = owner[None, :] == owner[:, None]
    rank = jnp.sum(jnp.where(before & same, 1, 0), axis=1)
    place = owner * 2 + rank
    matches = place[None, :] == jnp.arange(128)[:, None]
    ids = jnp.sum(jnp.where(matches, local[None, :], 0), axis=1)
    return ids.astype(jnp.int32)[None, :], jnp.stack([starts, place]).astype(jnp.int32)


def kernel(
    owners,
    groups,
    ids_ref,
    meta_ref,
    tokens_hbm,
    weight_hbm,
    down_hbm,
    up_hbm,
    out_ref,
    tokens,
    weight,
    down,
    up,
    stage,
    stage_up,
    held,
    held_up,
    base_send,
    base_held,
    acc,
    code,
    packed,
    packed_held,
    rounded,
    ids_all,
    ids_smem,
    load_sem,
    ids_send,
    ids_recv,
    down_send,
    down_recv,
    up_send,
    up_recv,
    base_ssem,
    base_rsem,
    part_ssem,
    part_rsem,
    full_ssem,
    full_rsem,
):
    me = lax.axis_index("wide")
    grp = lax.axis_index("grp")
    my_y, my_z = me // 8, me % 8
    my_x, core = grp // 2, grp % 2
    tokens_n = tokens.shape[0]
    steps = owners - 1

    def offset(i):
        zi, dy = i // 4, (i % 4 + 1) % 4
        dz = (4 - (zi + 1) // 2) * (2 * (zi % 2) - 1) * (1 - 2 * core)
        return dy, dz

    def target(i):
        dy, dz = offset(i)
        return ((my_y + dy) % 4) * 8 + (my_z + dz + 8) % 8

    def source(i):
        dy, dz = offset(i)
        return ((my_y - dy + 4) % 4) * 8 + (my_z - dz + 8) % 8

    loads = [
        pltpu.make_async_copy(down_hbm, down, load_sem.at[0]),
        pltpu.make_async_copy(up_hbm, up, load_sem.at[1]),
        pltpu.make_async_copy(tokens_hbm, tokens, load_sem.at[2]),
        pltpu.make_async_copy(weight_hbm, weight, load_sem.at[3]),
    ]
    for load in loads:
        load.start()
    own_ids = pltpu.make_async_copy(ids_ref, ids_all.at[me], load_sem.at[4])
    own_ids.start()

    barrier = pltpu.get_barrier_semaphore()

    @pl.loop(0, steps)
    def _(i):
        pl.semaphore_signal(barrier, 1, device_id=(target(i), grp), device_id_type=MESH)

    @pl.loop(1, groups)
    def _(k):
        pl.semaphore_signal(barrier, 1, device_id=(me, (grp + k) % groups), device_id_type=MESH)

    pl.semaphore_wait(barrier, steps + groups - 1)

    def ids_copy(i):
        return pltpu.make_async_remote_copy(
            ids_ref, ids_all.at[me], ids_send.at[i], ids_recv.at[i],
            device_id=(target(i), grp), device_id_type=MESH,
        )

    @pl.loop(0, steps)
    def _(i):
        ids_copy(i).start()

    own_ids.wait()

    def ids_arrival(i):
        return pltpu.make_async_remote_copy(
            ids_ref, ids_all.at[source(i)], ids_send.at[i], ids_recv.at[i],
            device_id=(target(i), grp), device_id_type=MESH,
        )

    @pl.loop(0, steps)
    def _(i):
        ids_arrival(i).wait()

    to_smem = pltpu.make_async_copy(ids_all, ids_smem, load_sem.at[5])
    to_smem.start()
    to_smem.wait()
    loads[0].wait()

    def down_copy(i):
        return pltpu.make_async_remote_copy(
            stage.at[i], held.at[i], down_send.at[i], down_recv.at[i],
            device_id=(target(i), grp), device_id_type=MESH,
        )

    def up_copy(i):
        return pltpu.make_async_remote_copy(
            stage_up.at[i], held_up.at[i], up_send.at[i], up_recv.at[i],
            device_id=(target(i), grp), device_id_type=MESH,
        )

    @pl.loop(0, steps)
    def _(i):
        to = target(i)
        stage[i, 0:64] = down[ids_smem[to, 0, 2 * me]]
        stage[i, 64:128] = down[ids_smem[to, 0, 2 * me + 1]]
        down_copy(i).start()

    held[steps, 0:64] = down[ids_smem[me, 0, 2 * me]]
    held[steps, 64:128] = down[ids_smem[me, 0, 2 * me + 1]]
    loads[1].wait()

    @pl.loop(0, steps)
    def _(i):
        to = target(i)
        stage_up[i, 0:64] = up[ids_smem[to, 0, 2 * me]]
        stage_up[i, 64:128] = up[ids_smem[to, 0, 2 * me + 1]]
        up_copy(i).start()

    held_up[steps, 0:64] = up[ids_smem[me, 0, 2 * me]]
    held_up[steps, 64:128] = up[ids_smem[me, 0, 2 * me + 1]]

    def base_copy(k, c):
        slot = 2 * k + c
        return pltpu.make_async_remote_copy(
            base_send.at[slot], base_held.at[2 * k + core], base_ssem.at[slot], base_rsem.at[2 * k + core],
            device_id=(me, ((my_x + k) % 4) * 2 + c), device_id_type=MESH,
        )

    def base_arrival(k, c):
        slot = 2 * k + c
        return pltpu.make_async_remote_copy(
            base_send.at[slot], base_held.at[slot], base_ssem.at[slot], base_rsem.at[slot],
            device_id=(me, ((my_x + k) % 4) * 2 + c), device_id_type=MESH,
        )

    loads[2].wait()
    loads[3].wait()

    @pl.loop(0, 4)
    def _(k):
        columns = pl.ds(pl.multiple_of(((my_x + k) % 4) * 256, 256), 256)

        @pl.loop(0, tokens_n // ROWS)
        def _(m):
            rows = pl.ds(pl.multiple_of(m * ROWS, ROWS), ROWS)
            part = jnp.dot(tokens[rows, :], weight[:, columns], preferred_element_type=F32)
            base_send[2 * k, rows] = part[:, :128]
            base_send[2 * k + 1, rows] = part[:, 128:]

        @pl.when(k == 0)
        def _():
            base_copy(0, 1 - core).start()

        @pl.when(k > 0)
        def _():
            base_copy(k, 0).start()
            base_copy(k, 1).start()

    lane = lax.broadcasted_iota(jnp.int32, (ROWS, 128), 1)
    row = lax.broadcasted_iota(jnp.int32, (ROWS, 128), 0)
    upper = jnp.where(lane < 64, 0, 1)

    @pl.loop(0, tokens_n // ROWS)
    def _(m):
        rows = pl.ds(pl.multiple_of(m * ROWS, ROWS), ROWS)
        at = row + m * ROWS
        slot = lax.fori_loop(
            0, meta_ref.shape[1],
            lambda r, s: jnp.where(at >= meta_ref[0, r], meta_ref[1, r], s),
            jnp.zeros((ROWS, 128), jnp.int32),
        )
        code[rows] = slot - upper
        acc[rows] = jnp.zeros((ROWS, 128), F32)

    @pl.loop(0, owners // 2)
    def _(j):
        down_copy(2 * j).wait_recv()

        @pl.when(2 * j + 1 < steps)
        def _():
            down_copy(2 * j + 1).wait_recv()

        first, second = 2 * source(2 * j), 2 * source(2 * j + 1)

        @pl.loop(0, tokens_n // ROWS)
        def _(m):
            rows = pl.ds(pl.multiple_of(m * ROWS, ROWS), ROWS)
            panels = held[pl.ds(2 * j, 2)].reshape(256, held.shape[2])
            part = lax.dot_general(
                tokens[rows, :], panels, (((1,), (1,)), ((), ())), preferred_element_type=F32
            )
            at = code[rows]
            acc[rows] += jnp.where(at == first, part[:, :128], 0.0) + jnp.where(at == second, part[:, 128:], 0.0)

    half = lax.broadcasted_iota(jnp.int32, (128, 128), 1) < 64

    @pl.loop(0, groups)
    def _(p):
        top = acc[pl.ds(pl.multiple_of(p * 256, 256), 128)]
        low = acc[pl.ds(pl.multiple_of(p * 256 + 128, 128), 128)]
        packed[p] = jnp.where(half, top + pltpu.roll(top, 64, 1), low + pltpu.roll(low, 64, 1))

    def part_copy(k):
        to = (grp + k) % groups
        return pltpu.make_async_remote_copy(
            packed.at[to], packed_held.at[k], part_ssem.at[k], part_rsem.at[k],
            device_id=(me, to), device_id_type=MESH,
        )

    @pl.loop(1, groups)
    def _(k):
        part_copy(k).start()

    @pl.loop(0, 4)
    def _(k):
        @pl.when(k == 0)
        def _():
            base_arrival(0, 1 - core).wait_recv()

        @pl.when(k > 0)
        def _():
            base_arrival(k, 0).wait_recv()
            base_arrival(k, 1).wait_recv()

    @pl.loop(0, tokens_n // ROWS)
    def _(m):
        rows = pl.ds(pl.multiple_of(m * ROWS, ROWS), ROWS)
        total = base_send[core, rows] + base_held[1 - core, rows]
        for slot in range(2, 8):
            total = total + base_held[slot, rows]
        base_held[core, rows] = total
        acc[rows] = jnp.zeros((ROWS, 128), F32)

    total = packed[grp]

    def add_part(k, s):
        part_copy(k).wait_recv()
        return s + packed_held[k]

    rounded[grp] = lax.fori_loop(1, groups, add_part, total).astype(BF16)

    def full_copy(k):
        return pltpu.make_async_remote_copy(
            rounded.at[grp], rounded.at[grp], full_ssem.at[k], full_rsem.at[k],
            device_id=(me, (grp + k) % groups), device_id_type=MESH,
        )

    def full_arrival(k):
        source_of = (grp + groups - k) % groups
        return pltpu.make_async_remote_copy(
            rounded.at[source_of], rounded.at[source_of], full_ssem.at[k], full_rsem.at[k],
            device_id=(me, (grp + k) % groups), device_id_type=MESH,
        )

    @pl.loop(1, groups)
    def _(k):
        full_copy(k).start()

    @pl.loop(1, groups)
    def _(k):
        full_arrival(k).wait_recv()

    shrunk = base_send.at[1 - core]

    @pl.loop(1, groups)
    def _(k):
        part_copy(k).wait_send()

    base_copy(0, 1 - core).wait_send()

    @pl.loop(0, groups)
    def _(p):
        both = rounded[p].astype(F32)
        other = pltpu.roll(both, 64, 1)
        shrunk[pl.ds(pl.multiple_of(p * 256, 256), 128)] = jnp.where(half, both, other)
        shrunk[pl.ds(pl.multiple_of(p * 256 + 128, 128), 128)] = jnp.where(half, other, both)

    @pl.loop(0, owners // 4)
    def _(j):
        for a in range(3):
            up_copy(4 * j + a).wait_recv()

        @pl.when(4 * j + 3 < steps)
        def _():
            up_copy(4 * j + 3).wait_recv()

        names = [2 * source(4 * j + a) for a in range(4)]

        @pl.loop(0, tokens_n // ROWS)
        def _(m):
            rows = pl.ds(pl.multiple_of(m * ROWS, ROWS), ROWS)
            at, value = code[rows], shrunk[rows]
            spread = jnp.concatenate([jnp.where(at == n, value, 0.0).astype(BF16) for n in names], axis=1)
            panels = held_up[pl.ds(4 * j, 4)].reshape(512, 128)
            acc[rows] += jnp.dot(spread, panels, preferred_element_type=F32)

    @pl.loop(0, tokens_n // ROWS)
    def _(m):
        rows = pl.ds(pl.multiple_of(m * ROWS, ROWS), ROWS)
        out_ref[rows] = (base_held[core, rows] + acc[rows].astype(BF16).astype(F32)).astype(BF16)

    @pl.loop(0, steps)
    def _(i):
        down_copy(i).wait_send()
        up_copy(i).wait_send()

    @pl.loop(1, groups)
    def _(k):
        full_copy(k).wait_send()

    @pl.loop(1, 4)
    def _(k):
        base_copy(k, 0).wait_send()
        base_copy(k, 1).wait_send()


def shards(tokens, value_weight, down_panels, up_panels, request_adapter, request_length, adapter_panel_place):
    owners, groups = lax.axis_size("wide"), lax.axis_size("grp")
    ids, meta = routes(request_adapter, request_length, adapter_panel_place)
    rows, features = tokens.shape
    units = up_panels.shape[2]
    dma = pltpu.SemaphoreType.DMA
    vmem = pltpu.VMEM
    return pl.pallas_call(
        functools.partial(kernel, owners, groups),
        out_shape=jax.ShapeDtypeStruct((rows, units), BF16),
        in_specs=[
            pl.BlockSpec(memory_space=pltpu.VMEM),
            pl.BlockSpec(memory_space=pltpu.SMEM),
        ]
        + [pl.BlockSpec(memory_space=pl.ANY)] * 4,
        out_specs=pl.BlockSpec(memory_space=pltpu.VMEM),
        scratch_shapes=[
            vmem(tokens.shape, BF16),
            vmem(value_weight.shape, BF16),
            vmem(down_panels.shape, BF16),
            vmem(up_panels.shape, BF16),
            vmem((owners - 1, 128, features), BF16),
            vmem((owners - 1, 128, units), BF16),
            vmem((owners, 128, features), BF16),
            vmem((owners, 128, units), BF16),
            vmem((groups, rows, units), F32),
            vmem((groups, rows, units), F32),
            vmem((rows, 128), F32),
            vmem((rows, 128), jnp.int32),
            vmem((groups, 128, 128), F32),
            vmem((groups, 128, 128), F32),
            vmem((groups, 128, 128), BF16),
            vmem((owners, 1, 128), jnp.int32),
            pltpu.SMEM((owners, 1, 128), jnp.int32),
            dma((6,)),
            dma((owners - 1,)),
            dma((owners - 1,)),
            dma((owners - 1,)),
            dma((owners - 1,)),
            dma((owners - 1,)),
            dma((owners - 1,)),
            dma((groups,)),
            dma((groups,)),
            dma((groups,)),
            dma((groups,)),
            dma((groups,)),
            dma((groups,)),
        ],
        compiler_params=pltpu.CompilerParams(
            collective_id=0, has_side_effects=True, vmem_limit_bytes=60 * 2**20
        ),
        name="routed_lora",
    )(ids, meta, tokens, value_weight, down_panels, up_panels)


def solution(mesh):
    placed = (
        P("wide", "grp"),
        P("grp", None),
        P("wide", None, "grp"),
        P("wide", None, "grp"),
        P("wide", None),
        P("wide", None),
        P(),
    )
    return jax.shard_map(
        shards, mesh=mesh, in_specs=placed, out_specs=P("wide", "grp"), check_vma=False
    )
```

```python
import functools

import jax
import jax.numpy as jnp
from jax import lax
from jax.experimental import pallas as pl
from jax.experimental.pallas import tpu as pltpu
from jax.sharding import PartitionSpec as P

MESH = pl.DeviceIdType.MESH
ADP_W = 40
F32 = jnp.float32
BF16 = jnp.bfloat16
ROWS = 512


def kernel(
    owners,
    groups,
    adapter_ref,
    length_ref,
    place_ref,
    tokens_hbm,
    weight_hbm,
    down_hbm,
    up_hbm,
    out_ref,
    tokens,
    weight,
    down,
    up,
    stage,
    stage_up,
    held,
    held_up,
    base_send,
    base_held,
    acc,
    code,
    packed,
    packed_held,
    rounded,
    ids_ref,
    ids_all,
    ids_smem,
    meta_ref,
    load_sem,
    ids_send,
    ids_recv,
    down_send,
    down_recv,
    up_send,
    up_recv,
    base_ssem,
    base_rsem,
    part_ssem,
    part_rsem,
    full_ssem,
    full_rsem,
):
    me = lax.axis_index("wide")
    grp = lax.axis_index("grp")
    my_y, my_z = me // 8, me % 8
    my_x, core = grp // 2, grp % 2
    tokens_n = tokens.shape[0]
    steps = owners - 1

    def offset(i):
        n = i % 8
        dy = (i // 8 + n + 2) % 4
        dz = (4 - n + 3 * (n // 4)) * (1 - 2 * (n % 2)) * (1 - 2 * core)
        return dy, dz

    def target(i):
        dy, dz = offset(i)
        return ((my_y + dy) % 4) * 8 + (my_z + dz + 8) % 8

    def source(i):
        dy, dz = offset(i)
        return ((my_y - dy + 4) % 4) * 8 + (my_z - dz + 8) % 8

    loads = [
        pltpu.make_async_copy(down_hbm, down, load_sem.at[0]),
        pltpu.make_async_copy(up_hbm, up, load_sem.at[1]),
        pltpu.make_async_copy(tokens_hbm, tokens, load_sem.at[2]),
        pltpu.make_async_copy(weight_hbm, weight, load_sem.at[3]),
    ]
    for load in loads:
        load.start()

    barrier = pltpu.get_barrier_semaphore()

    @pl.loop(0, steps)
    def _(i):
        pl.semaphore_signal(barrier, 1, device_id=(target(i), grp), device_id_type=MESH)

    @pl.loop(1, groups)
    def _(k):
        pl.semaphore_signal(barrier, 1, device_id=(me, (grp + k) % groups), device_id_type=MESH)

    lanes = lax.broadcasted_iota(jnp.int32, (1, 128), 1)
    lane_owner, lane_turn = lanes // 2, lanes % 2
    count = adapter_ref.shape[1]

    def route(r, state):
        ids, turn, start = state
        panel = place_ref[adapter_ref[0, r]]
        owner = panel // ADP_W
        meta_ref[0, r] = start
        meta_ref[1, r] = owner
        hit = lane_owner == owner
        ids = jnp.where(hit & (lane_turn == turn), panel - owner * ADP_W, ids)
        return ids, jnp.where(hit, turn + 1, turn), start + length_ref[0, r]

    nothing = jnp.zeros((1, 128), jnp.int32)
    ids_ref[...] = lax.fori_loop(0, count, route, (nothing, nothing, 0))[0]
    own_ids = pltpu.make_async_copy(ids_ref, ids_all.at[me], load_sem.at[4])
    own_ids.start()
    pl.semaphore_wait(barrier, steps + groups - 1)

    def ids_copy(i):
        return pltpu.make_async_remote_copy(
            ids_ref, ids_all.at[me], ids_send.at[i], ids_recv.at[i],
            device_id=(target(i), grp), device_id_type=MESH,
        )

    @pl.loop(0, steps)
    def _(i):
        ids_copy(i).start()

    own_ids.wait()

    def ids_arrival(i):
        return pltpu.make_async_remote_copy(
            ids_ref, ids_all.at[source(i)], ids_send.at[i], ids_recv.at[i],
            device_id=(target(i), grp), device_id_type=MESH,
        )

    @pl.loop(0, steps)
    def _(i):
        ids_arrival(i).wait()

    to_smem = pltpu.make_async_copy(ids_all, ids_smem, load_sem.at[5])
    to_smem.start()
    to_smem.wait()
    loads[0].wait()

    def down_copy(i):
        return pltpu.make_async_remote_copy(
            stage.at[i], held.at[i], down_send.at[i], down_recv.at[i],
            device_id=(target(i), grp), device_id_type=MESH,
        )

    def up_copy(i):
        return pltpu.make_async_remote_copy(
            stage_up.at[i], held_up.at[i], up_send.at[i], up_recv.at[i],
            device_id=(target(i), grp), device_id_type=MESH,
        )

    @pl.loop(0, steps)
    def _(i):
        to = target(i)
        stage[i, 0:64] = down[ids_smem[to, 0, 2 * me]]
        stage[i, 64:128] = down[ids_smem[to, 0, 2 * me + 1]]
        down_copy(i).start()

    held[steps, 0:64] = down[ids_smem[me, 0, 2 * me]]
    held[steps, 64:128] = down[ids_smem[me, 0, 2 * me + 1]]
    loads[1].wait()

    @pl.loop(0, steps)
    def _(i):
        to = target(i)
        stage_up[i, 0:64] = up[ids_smem[to, 0, 2 * me]]
        stage_up[i, 64:128] = up[ids_smem[to, 0, 2 * me + 1]]
        up_copy(i).start()

    held_up[steps, 0:64] = up[ids_smem[me, 0, 2 * me]]
    held_up[steps, 64:128] = up[ids_smem[me, 0, 2 * me + 1]]

    def base_copy(k, c):
        slot = 2 * k + c
        return pltpu.make_async_remote_copy(
            base_send.at[slot], base_held.at[2 * k + core], base_ssem.at[slot], base_rsem.at[2 * k + core],
            device_id=(me, ((my_x + k) % 4) * 2 + c), device_id_type=MESH,
        )

    def base_arrival(k, c):
        slot = 2 * k + c
        return pltpu.make_async_remote_copy(
            base_send.at[slot], base_held.at[slot], base_ssem.at[slot], base_rsem.at[slot],
            device_id=(me, ((my_x + k) % 4) * 2 + c), device_id_type=MESH,
        )

    loads[2].wait()
    loads[3].wait()

    @pl.loop(0, 4)
    def _(k):
        columns = pl.ds(pl.multiple_of(((my_x + k) % 4) * 256, 256), 256)

        @pl.loop(0, tokens_n // ROWS)
        def _(m):
            rows = pl.ds(pl.multiple_of(m * ROWS, ROWS), ROWS)
            part = jnp.dot(tokens[rows, :], weight[:, columns], preferred_element_type=F32)
            base_send[2 * k, rows] = part[:, :128]
            base_send[2 * k + 1, rows] = part[:, 128:]

        @pl.when(k == 0)
        def _():
            base_copy(0, 1 - core).start()

        @pl.when(k > 0)
        def _():
            base_copy(k, 0).start()
            base_copy(k, 1).start()

    lane = lax.broadcasted_iota(jnp.int32, (ROWS, 128), 1)
    row = lax.broadcasted_iota(jnp.int32, (ROWS, 128), 0)
    upper = jnp.where(lane < 64, 0, 1)

    @pl.loop(0, count)
    def _(r):
        def earlier(q, rank):
            return rank + jnp.where((meta_ref[1, q] == meta_ref[1, r]) & (q < r), 1, 0)

        meta_ref[2, r] = 2 * meta_ref[1, r] + lax.fori_loop(0, count, earlier, 0)

    @pl.loop(0, tokens_n // ROWS)
    def _(m):
        rows = pl.ds(pl.multiple_of(m * ROWS, ROWS), ROWS)
        at = row + m * ROWS
        slot = lax.fori_loop(
            0, count,
            lambda r, s: jnp.where(at >= meta_ref[0, r], meta_ref[2, r], s),
            jnp.zeros((ROWS, 128), jnp.int32),
        )
        code[rows] = slot - upper
        acc[rows] = jnp.zeros((ROWS, 128), F32)

    def shrink(j):
        down_copy(2 * j).wait_recv()

        @pl.when(2 * j + 1 < steps)
        def _():
            down_copy(2 * j + 1).wait_recv()

        first, second = 2 * source(2 * j), 2 * source(2 * j + 1)

        @pl.loop(0, tokens_n // 1024)
        def _(m):
            rows = pl.ds(pl.multiple_of(m * 1024, 1024), 1024)
            panels = held[pl.ds(2 * j, 2)].reshape(256, held.shape[2])
            part = lax.dot_general(
                tokens[rows, :], panels, (((1,), (1,)), ((), ())), preferred_element_type=F32
            )
            at = code[rows]
            acc[rows] += jnp.where(at == first, part[:, :128], 0.0) + jnp.where(at == second, part[:, 128:], 0.0)

    @pl.loop(0, owners // 2 - 4)
    def _(j):
        shrink(j)

    base_arrival(0, 1 - core).wait_recv()

    @pl.loop(1, 4)
    def _(k):
        base_arrival(k, 0).wait_recv()
        base_arrival(k, 1).wait_recv()

    @pl.loop(0, tokens_n // 256)
    def _(m):
        rows = pl.ds(pl.multiple_of(m * 256, 256), 256)
        total = base_send[core, rows] + base_held[1 - core, rows]
        for slot in range(2, 8):
            total = total + base_held[slot, rows]
        base_held[core, rows] = total

    @pl.loop(owners // 2 - 4, owners // 2)
    def _(j):
        shrink(j)

    half = lax.broadcasted_iota(jnp.int32, (128, 128), 1) < 64

    def pack(k):
        p = (grp + k) % groups
        top = acc[pl.ds(pl.multiple_of(p * 256, 256), 128)]
        low = acc[pl.ds(pl.multiple_of(p * 256 + 128, 128), 128)]
        packed[k] = jnp.where(half, top + pltpu.roll(top, 64, 1), low + pltpu.roll(low, 64, 1))

    def part_copy(k):
        return pltpu.make_async_remote_copy(
            packed.at[k], packed_held.at[k], part_ssem.at[k], part_rsem.at[k],
            device_id=(me, (grp + k) % groups), device_id_type=MESH,
        )

    @pl.loop(1, groups)
    def _(k):
        pack(k)
        part_copy(k).start()

    pack(0)

    @pl.loop(0, tokens_n // ROWS)
    def _(m):
        rows = pl.ds(pl.multiple_of(m * ROWS, ROWS), ROWS)
        acc[rows] = jnp.zeros((ROWS, 128), F32)

    total = packed[0]

    def add_part(k, s):
        part_copy(k).wait_recv()
        return s + packed_held[k]

    rounded[0] = lax.fori_loop(1, groups, add_part, total).astype(BF16)

    def full_copy(k):
        return pltpu.make_async_remote_copy(
            rounded.at[0], rounded.at[k], full_ssem.at[k], full_rsem.at[k],
            device_id=(me, (grp + k) % groups), device_id_type=MESH,
        )

    @pl.loop(1, groups)
    def _(k):
        full_copy(k).start()

    shrunk = base_send.at[1 - core]
    base_copy(0, 1 - core).wait_send()

    @pl.loop(1, 4)
    def _(k):
        base_copy(k, 0).wait_send()
        base_copy(k, 1).wait_send()

    def unpack(k):
        p = (grp + groups - k) % groups
        both = rounded[k].astype(F32)
        other = pltpu.roll(both, 64, 1)
        shrunk[pl.ds(pl.multiple_of(p * 256, 256), 128)] = jnp.where(half, both, other)
        shrunk[pl.ds(pl.multiple_of(p * 256 + 128, 128), 128)] = jnp.where(half, other, both)

    unpack(0)

    @pl.loop(1, groups)
    def _(k):
        full_copy(k).wait_recv()
        unpack(k)

    def apply(j):
        @pl.loop(0, 8)
        def _(a):
            @pl.when(8 * j + a < steps)
            def _():
                up_copy(8 * j + a).wait_recv()

        names = [2 * source(8 * j + a) for a in range(8)]

        @pl.loop(0, tokens_n // ROWS)
        def _(m):
            rows = pl.ds(pl.multiple_of(m * ROWS, ROWS), ROWS)
            at, value = code[rows], shrunk[rows]
            spread = jnp.concatenate([jnp.where(at == n, value, 0.0).astype(BF16) for n in names], axis=1)
            panels = held_up[pl.ds(8 * j, 8)].reshape(8 * 128, 128)
            acc[rows] += jnp.dot(spread, panels, preferred_element_type=F32)

    @pl.loop(0, owners // 8)
    def _(j):
        apply(j)

    @pl.loop(0, tokens_n // ROWS)
    def _(m):
        rows = pl.ds(pl.multiple_of(m * ROWS, ROWS), ROWS)
        out_ref[rows] = (base_held[core, rows] + acc[rows].astype(BF16).astype(F32)).astype(BF16)

    @pl.loop(0, steps)
    def _(i):
        down_copy(i).wait_send()
        up_copy(i).wait_send()

    @pl.loop(1, groups)
    def _(k):
        part_copy(k).wait_send()
        full_copy(k).wait_send()


def shards(tokens, value_weight, down_panels, up_panels, request_adapter, request_length, adapter_panel_place):
    owners, groups = lax.axis_size("wide"), lax.axis_size("grp")
    rows, features = tokens.shape
    units = up_panels.shape[2]
    dma = pltpu.SemaphoreType.DMA
    vmem = pltpu.VMEM
    return pl.pallas_call(
        functools.partial(kernel, owners, groups),
        out_shape=jax.ShapeDtypeStruct((rows, units), BF16),
        in_specs=[
            pl.BlockSpec(memory_space=pltpu.SMEM),
            pl.BlockSpec(memory_space=pltpu.SMEM),
            pl.BlockSpec(memory_space=pltpu.SMEM),
        ]
        + [pl.BlockSpec(memory_space=pl.ANY)] * 4,
        out_specs=pl.BlockSpec(memory_space=pltpu.VMEM),
        scratch_shapes=[
            vmem(tokens.shape, BF16),
            vmem(value_weight.shape, BF16),
            vmem(down_panels.shape, BF16),
            vmem(up_panels.shape, BF16),
            vmem((owners - 1, 128, features), BF16),
            vmem((owners - 1, 128, units), BF16),
            vmem((owners, 128, features), BF16),
            vmem((owners, 128, units), BF16),
            vmem((groups, rows, units), F32),
            vmem((groups, rows, units), F32),
            vmem((rows, 128), F32),
            vmem((rows, 128), jnp.int32),
            vmem((groups, 128, 128), F32),
            vmem((groups, 128, 128), F32),
            vmem((groups, 128, 128), BF16),
            vmem((1, 128), jnp.int32),
            vmem((owners, 1, 128), jnp.int32),
            pltpu.SMEM((owners, 1, 128), jnp.int32),
            pltpu.SMEM((3, request_adapter.shape[1]), jnp.int32),
            dma((6,)),
            dma((owners - 1,)),
            dma((owners - 1,)),
            dma((owners - 1,)),
            dma((owners - 1,)),
            dma((owners - 1,)),
            dma((owners - 1,)),
            dma((groups,)),
            dma((groups,)),
            dma((groups,)),
            dma((groups,)),
            dma((groups,)),
            dma((groups,)),
        ],
        compiler_params=pltpu.CompilerParams(
            collective_id=0, has_side_effects=True, vmem_limit_bytes=60 * 2**20
        ),
        name="routed_lora",
    )(request_adapter, request_length, adapter_panel_place, tokens, value_weight, down_panels, up_panels)


def solution(mesh):
    placed = (
        P("wide", "grp"),
        P("grp", None),
        P("wide", None, "grp"),
        P("wide", None, "grp"),
        P("wide", None),
        P("wide", None),
        P(),
    )
    return jax.shard_map(
        shards, mesh=mesh, in_specs=placed, out_specs=P("wide", "grp"), check_vma=False
    )
```

```python
import functools

import jax
import jax.numpy as jnp
from jax import lax
from jax.experimental import pallas as pl
from jax.experimental.pallas import tpu as pltpu
from jax.sharding import PartitionSpec as P

MESH = pl.DeviceIdType.MESH
ADP_W = 40
F32 = jnp.float32
BF16 = jnp.bfloat16
ROWS = 1024


def kernel(
    owners,
    groups,
    adapter_hbm,
    length_hbm,
    place_hbm,
    tokens_hbm,
    weight_hbm,
    down_hbm,
    up_hbm,
    out_ref,
    tokens,
    weight,
    down,
    up,
    stage,
    stage_up,
    held,
    held_up,
    base_send,
    base_held,
    acc,
    code,
    packed,
    packed_held,
    rounded,
    adapter_ref,
    length_ref,
    place_ref,
    ids_ref,
    ids_all,
    ids_smem,
    meta_ref,
    load_sem,
    ids_send,
    ids_recv,
    down_send,
    down_recv,
    up_send,
    up_recv,
    base_ssem,
    base_rsem,
    part_ssem,
    part_rsem,
    full_ssem,
    full_rsem,
):
    me = lax.axis_index("wide")
    grp = lax.axis_index("grp")
    my_y, my_z = me // 8, me % 8
    my_x, core = grp // 2, grp % 2
    tokens_n = tokens.shape[0]
    steps = owners - 1

    def offset(i):
        n = i % 8
        dy = (i // 8 + n + 2) % 4
        dz = (4 - n + 3 * (n // 4)) * (1 - 2 * (n % 2)) * (1 - 2 * core)
        return dy, dz

    def target(i):
        dy, dz = offset(i)
        return ((my_y + dy) % 4) * 8 + (my_z + dz + 8) % 8

    def source(i):
        dy, dz = offset(i)
        return ((my_y - dy + 4) % 4) * 8 + (my_z - dz + 8) % 8

    tables = [
        pltpu.make_async_copy(adapter_hbm, adapter_ref, load_sem.at[6]),
        pltpu.make_async_copy(length_hbm, length_ref, load_sem.at[7]),
        pltpu.make_async_copy(place_hbm, place_ref, load_sem.at[8]),
    ]
    for table in tables:
        table.start()
    loads = [
        pltpu.make_async_copy(down_hbm, down, load_sem.at[0]),
        pltpu.make_async_copy(up_hbm, up, load_sem.at[1]),
        pltpu.make_async_copy(tokens_hbm, tokens, load_sem.at[2]),
        pltpu.make_async_copy(weight_hbm, weight, load_sem.at[3]),
    ]
    for load in loads:
        load.start()

    barrier = pltpu.get_barrier_semaphore()

    for i in range(steps):
        pl.semaphore_signal(barrier, 1, device_id=(target(i), grp), device_id_type=MESH)

    @pl.loop(1, groups)
    def _(k):
        pl.semaphore_signal(barrier, 1, device_id=(me, (grp + k) % groups), device_id_type=MESH)

    lanes = lax.broadcasted_iota(jnp.int32, (1, 128), 1)
    lane_owner, lane_turn = lanes // 2, lanes % 2
    count = adapter_ref.shape[1]

    def route(r, state):
        ids, turn, start = state
        panel = place_ref[adapter_ref[0, r]]
        owner = panel // ADP_W
        meta_ref[0, r] = start
        meta_ref[1, r] = owner
        hit = lane_owner == owner
        ids = jnp.where(hit & (lane_turn == turn), panel - owner * ADP_W, ids)
        return ids, jnp.where(hit, turn + 1, turn), start + length_ref[0, r]

    for table in tables:
        table.wait()
    nothing = jnp.zeros((1, 128), jnp.int32)
    ids_ref[...] = lax.fori_loop(0, count, route, (nothing, nothing, 0))[0]
    own_ids = pltpu.make_async_copy(ids_ref, ids_all.at[me], load_sem.at[4])
    own_ids.start()
    pl.semaphore_wait(barrier, steps + groups - 1)

    def ids_copy(i):
        return pltpu.make_async_remote_copy(
            ids_ref, ids_all.at[me], ids_send.at[i], ids_recv.at[i],
            device_id=(target(i), grp), device_id_type=MESH,
        )

    for i in range(steps):
        ids_copy(i).start()

    own_ids.wait()

    def ids_arrival(i):
        return pltpu.make_async_remote_copy(
            ids_ref, ids_all.at[source(i)], ids_send.at[i], ids_recv.at[i],
            device_id=(target(i), grp), device_id_type=MESH,
        )

    for i in range(steps):
        ids_arrival(i).wait()

    to_smem = pltpu.make_async_copy(ids_all, ids_smem, load_sem.at[5])
    to_smem.start()
    to_smem.wait()
    loads[0].wait()

    def down_copy(i):
        return pltpu.make_async_remote_copy(
            stage.at[i], held.at[i], down_send.at[i], down_recv.at[i],
            device_id=(target(i), grp), device_id_type=MESH,
        )

    def up_copy(i):
        return pltpu.make_async_remote_copy(
            stage_up.at[i], held_up.at[i], up_send.at[i], up_recv.at[i],
            device_id=(target(i), grp), device_id_type=MESH,
        )

    @pl.loop(0, steps)
    def _(i):
        to = target(i)
        stage[i, 0:64] = down[ids_smem[to, 0, 2 * me]]
        stage[i, 64:128] = down[ids_smem[to, 0, 2 * me + 1]]
        down_copy(i).start()

    held[steps, 0:64] = down[ids_smem[me, 0, 2 * me]]
    held[steps, 64:128] = down[ids_smem[me, 0, 2 * me + 1]]
    loads[1].wait()

    @pl.loop(0, steps)
    def _(i):
        to = target(i)
        stage_up[i, 0:64] = up[ids_smem[to, 0, 2 * me]]
        stage_up[i, 64:128] = up[ids_smem[to, 0, 2 * me + 1]]
        up_copy(i).start()

    held_up[steps, 0:64] = up[ids_smem[me, 0, 2 * me]]
    held_up[steps, 64:128] = up[ids_smem[me, 0, 2 * me + 1]]

    def base_copy(k, c):
        slot = 2 * k + c
        return pltpu.make_async_remote_copy(
            base_send.at[slot], base_held.at[2 * k + core], base_ssem.at[slot], base_rsem.at[2 * k + core],
            device_id=(me, ((my_x + k) % 4) * 2 + c), device_id_type=MESH,
        )

    def base_arrival(k, c):
        slot = 2 * k + c
        return pltpu.make_async_remote_copy(
            base_send.at[slot], base_held.at[slot], base_ssem.at[slot], base_rsem.at[slot],
            device_id=(me, ((my_x + k) % 4) * 2 + c), device_id_type=MESH,
        )

    loads[2].wait()
    loads[3].wait()

    @pl.loop(0, 4)
    def _(k):
        columns = pl.ds(pl.multiple_of(((my_x + k) % 4) * 256, 256), 256)

        @pl.loop(0, tokens_n // ROWS)
        def _(m):
            rows = pl.ds(pl.multiple_of(m * ROWS, ROWS), ROWS)
            part = jnp.dot(tokens[rows, :], weight[:, columns], preferred_element_type=F32)
            base_send[2 * k, rows] = part[:, :128]
            base_send[2 * k + 1, rows] = part[:, 128:]

        @pl.when(k == 0)
        def _():
            base_copy(0, 1 - core).start()

        @pl.when(k > 0)
        def _():
            base_copy(k, 0).start()
            base_copy(k, 1).start()

    lane = lax.broadcasted_iota(jnp.int32, (ROWS, 128), 1)
    row = lax.broadcasted_iota(jnp.int32, (ROWS, 128), 0)
    upper = jnp.where(lane < 64, 0, 1)

    @pl.loop(0, count)
    def _(r):
        def earlier(q, rank):
            return rank + jnp.where((meta_ref[1, q] == meta_ref[1, r]) & (q < r), 1, 0)

        meta_ref[2, r] = 2 * meta_ref[1, r] + lax.fori_loop(0, count, earlier, 0)

    @pl.loop(0, tokens_n // ROWS)
    def _(m):
        rows = pl.ds(pl.multiple_of(m * ROWS, ROWS), ROWS)
        at = row + m * ROWS
        slot = lax.fori_loop(
            0, count,
            lambda r, s: jnp.where(at >= meta_ref[0, r], meta_ref[2, r], s),
            jnp.zeros((ROWS, 128), jnp.int32),
        )
        code[rows] = slot - upper
        acc[rows] = jnp.zeros((ROWS, 128), F32)

    def shrink(j):
        down_copy(2 * j).wait_recv()

        @pl.when(2 * j + 1 < steps)
        def _():
            down_copy(2 * j + 1).wait_recv()

        first, second = 2 * source(2 * j), 2 * source(2 * j + 1)

        @pl.loop(0, tokens_n // 1024)
        def _(m):
            rows = pl.ds(pl.multiple_of(m * 1024, 1024), 1024)
            panels = held[pl.ds(2 * j, 2)].reshape(256, held.shape[2])
            part = lax.dot_general(
                tokens[rows, :], panels, (((1,), (1,)), ((), ())), preferred_element_type=F32
            )
            at = code[rows]
            acc[rows] += jnp.where(at == first, part[:, :128], 0.0) + jnp.where(at == second, part[:, 128:], 0.0)

    @pl.loop(0, owners // 2 - 4)
    def _(j):
        shrink(j)

    base_arrival(0, 1 - core).wait_recv()

    @pl.loop(1, 4)
    def _(k):
        base_arrival(k, 0).wait_recv()
        base_arrival(k, 1).wait_recv()

    @pl.loop(0, tokens_n // 256)
    def _(m):
        rows = pl.ds(pl.multiple_of(m * 256, 256), 256)
        total = base_send[core, rows] + base_held[1 - core, rows]
        for slot in range(2, 8):
            total = total + base_held[slot, rows]
        base_held[core, rows] = total

    @pl.loop(owners // 2 - 4, owners // 2)
    def _(j):
        shrink(j)

    half = lax.broadcasted_iota(jnp.int32, (128, 128), 1) < 64

    def pack(k):
        p = (grp + k) % groups
        top = acc[pl.ds(pl.multiple_of(p * 256, 256), 128)]
        low = acc[pl.ds(pl.multiple_of(p * 256 + 128, 128), 128)]
        packed[k] = jnp.where(half, top + pltpu.roll(top, 64, 1), low + pltpu.roll(low, 64, 1))

    def part_copy(k):
        return pltpu.make_async_remote_copy(
            packed.at[k], packed_held.at[k], part_ssem.at[k], part_rsem.at[k],
            device_id=(me, (grp + k) % groups), device_id_type=MESH,
        )

    @pl.loop(1, groups)
    def _(k):
        pack(k)
        part_copy(k).start()

    pack(0)

    @pl.loop(0, tokens_n // ROWS)
    def _(m):
        rows = pl.ds(pl.multiple_of(m * ROWS, ROWS), ROWS)
        acc[rows] = jnp.zeros((ROWS, 128), F32)

    total = packed[0]

    def add_part(k, s):
        part_copy(k).wait_recv()
        return s + packed_held[k]

    rounded[0] = lax.fori_loop(1, groups, add_part, total).astype(BF16)

    def full_copy(k):
        return pltpu.make_async_remote_copy(
            rounded.at[0], rounded.at[k], full_ssem.at[k], full_rsem.at[k],
            device_id=(me, (grp + k) % groups), device_id_type=MESH,
        )

    @pl.loop(1, groups)
    def _(k):
        full_copy(k).start()

    shrunk = base_send.at[1 - core]
    base_copy(0, 1 - core).wait_send()

    @pl.loop(1, 4)
    def _(k):
        base_copy(k, 0).wait_send()
        base_copy(k, 1).wait_send()

    def unpack(k):
        p = (grp + groups - k) % groups
        both = rounded[k].astype(F32)
        other = pltpu.roll(both, 64, 1)
        shrunk[pl.ds(pl.multiple_of(p * 256, 256), 128)] = jnp.where(half, both, other)
        shrunk[pl.ds(pl.multiple_of(p * 256 + 128, 128), 128)] = jnp.where(half, other, both)

    unpack(0)

    @pl.loop(1, groups)
    def _(k):
        full_copy(k).wait_recv()
        unpack(k)

    def arrive(first, count_up):
        @pl.loop(0, count_up)
        def _(a):
            @pl.when(first + a < steps)
            def _():
                up_copy(first + a).wait_recv()

    def term(first, count_up, rows):
        names = [2 * source(first + a) for a in range(count_up)]
        at, value = code[rows], shrunk[rows]
        spread = jnp.concatenate([jnp.where(at == n, value, 0.0).astype(BF16) for n in names], axis=1)
        panels = held_up[pl.ds(first, count_up)].reshape(count_up * 128, 128)
        return jnp.dot(spread, panels, preferred_element_type=F32)

    @pl.loop(0, owners // 8 - 1)
    def _(j):
        arrive(8 * j, 8)

        @pl.loop(0, tokens_n // ROWS)
        def _(m):
            rows = pl.ds(pl.multiple_of(m * ROWS, ROWS), ROWS)
            acc[rows] += term(8 * j, 8, rows)

    arrive(owners - 8, 8)

    @pl.loop(0, tokens_n // ROWS)
    def _(m):
        rows = pl.ds(pl.multiple_of(m * ROWS, ROWS), ROWS)
        delta = acc[rows] + term(owners - 8, 8, rows)
        out_ref[rows] = (base_held[core, rows] + delta.astype(BF16).astype(F32)).astype(BF16)

    @pl.loop(0, steps)
    def _(i):
        down_copy(i).wait_send()
        up_copy(i).wait_send()

    @pl.loop(1, groups)
    def _(k):
        part_copy(k).wait_send()
        full_copy(k).wait_send()


def shards(tokens, value_weight, down_panels, up_panels, request_adapter, request_length, adapter_panel_place):
    owners, groups = lax.axis_size("wide"), lax.axis_size("grp")
    rows, features = tokens.shape
    units = up_panels.shape[2]
    dma = pltpu.SemaphoreType.DMA
    vmem = pltpu.VMEM
    return pl.pallas_call(
        functools.partial(kernel, owners, groups),
        out_shape=jax.ShapeDtypeStruct((rows, units), BF16),
        in_specs=[pl.BlockSpec(memory_space=pl.ANY)] * 7,
        out_specs=pl.BlockSpec(memory_space=pltpu.VMEM),
        scratch_shapes=[
            vmem(tokens.shape, BF16),
            vmem(value_weight.shape, BF16),
            vmem(down_panels.shape, BF16),
            vmem(up_panels.shape, BF16),
            vmem((owners - 1, 128, features), BF16),
            vmem((owners - 1, 128, units), BF16),
            vmem((owners, 128, features), BF16),
            vmem((owners, 128, units), BF16),
            vmem((groups, rows, units), F32),
            vmem((groups, rows, units), F32),
            vmem((rows, 128), F32),
            vmem((rows, 128), jnp.int32),
            vmem((groups, 128, 128), F32),
            vmem((groups, 128, 128), F32),
            vmem((groups, 128, 128), BF16),
            pltpu.SMEM(request_adapter.shape, jnp.int32),
            pltpu.SMEM(request_length.shape, jnp.int32),
            pltpu.SMEM(adapter_panel_place.shape, jnp.int32),
            vmem((1, 128), jnp.int32),
            vmem((owners, 1, 128), jnp.int32),
            pltpu.SMEM((owners, 1, 128), jnp.int32),
            pltpu.SMEM((3, request_adapter.shape[1]), jnp.int32),
            dma((9,)),
            dma((owners - 1,)),
            dma((owners - 1,)),
            dma((owners - 1,)),
            dma((owners - 1,)),
            dma((owners - 1,)),
            dma((owners - 1,)),
            dma((groups,)),
            dma((groups,)),
            dma((groups,)),
            dma((groups,)),
            dma((groups,)),
            dma((groups,)),
        ],
        compiler_params=pltpu.CompilerParams(
            collective_id=0, has_side_effects=True, vmem_limit_bytes=60 * 2**20
        ),
        name="routed_lora",
    )(request_adapter, request_length, adapter_panel_place, tokens, value_weight, down_panels, up_panels)


def solution(mesh):
    placed = (
        P("wide", "grp"),
        P("grp", None),
        P("wide", None, "grp"),
        P("wide", None, "grp"),
        P("wide", None),
        P("wide", None),
        P(),
    )
    return jax.shard_map(
        shards, mesh=mesh, in_specs=placed, out_specs=P("wide", "grp"), check_vma=False
    )
```

```python
import functools

import jax
import jax.numpy as jnp
from jax import lax
from jax.experimental import pallas as pl
from jax.experimental.pallas import tpu as pltpu
from jax.sharding import PartitionSpec as P

MESH = pl.DeviceIdType.MESH
ADP_W = 40
F32 = jnp.float32
BF16 = jnp.bfloat16
ROWS = 1024


def kernel(
    owners,
    groups,
    adapter_hbm,
    length_hbm,
    place_hbm,
    tokens_hbm,
    weight_hbm,
    down_hbm,
    up_hbm,
    out_ref,
    tokens,
    weight,
    down,
    up,
    stage,
    stage_up,
    held,
    held_up,
    base_send,
    base_held,
    acc,
    code,
    packed,
    packed_held,
    rounded,
    adapter_ref,
    length_ref,
    place_ref,
    ids_ref,
    ids_all,
    ids_smem,
    meta_ref,
    load_sem,
    ids_send,
    ids_recv,
    down_send,
    down_recv,
    up_send,
    up_recv,
    base_ssem,
    base_rsem,
    part_ssem,
    part_rsem,
    full_ssem,
    full_rsem,
):
    me = lax.axis_index("wide")
    grp = lax.axis_index("grp")
    my_y, my_z = me // 8, me % 8
    my_x, core = grp // 2, grp % 2
    tokens_n = tokens.shape[0]
    steps = owners - 1

    def offset(i):
        n = i % 8
        dy = (i // 8 + n + 2) % 4
        dz = (4 - n + 3 * (n // 4)) * (1 - 2 * (n % 2)) * (1 - 2 * core)
        return dy, dz

    def target(i):
        dy, dz = offset(i)
        return ((my_y + dy) % 4) * 8 + (my_z + dz + 8) % 8

    def source(i):
        dy, dz = offset(i)
        return ((my_y - dy + 4) % 4) * 8 + (my_z - dz + 8) % 8

    tables = [
        pltpu.make_async_copy(adapter_hbm, adapter_ref, load_sem.at[6]),
        pltpu.make_async_copy(length_hbm, length_ref, load_sem.at[7]),
        pltpu.make_async_copy(place_hbm, place_ref, load_sem.at[8]),
    ]
    for table in tables:
        table.start()
    loads = [
        pltpu.make_async_copy(down_hbm, down, load_sem.at[0]),
        pltpu.make_async_copy(up_hbm, up, load_sem.at[1]),
        pltpu.make_async_copy(tokens_hbm, tokens, load_sem.at[2]),
        pltpu.make_async_copy(weight_hbm, weight, load_sem.at[3]),
    ]
    for load in loads:
        load.start()

    barrier = pltpu.get_barrier_semaphore()

    for i in range(steps):
        pl.semaphore_signal(barrier, 1, device_id=(target(i), grp), device_id_type=MESH)

    @pl.loop(1, groups)
    def _(k):
        pl.semaphore_signal(barrier, 1, device_id=(me, (grp + k) % groups), device_id_type=MESH)

    lanes = lax.broadcasted_iota(jnp.int32, (1, 128), 1)
    lane_owner, lane_turn = lanes // 2, lanes % 2
    count = adapter_ref.shape[1]

    def route(r, state):
        ids, turn, start = state
        panel = place_ref[adapter_ref[0, r]]
        owner = panel // ADP_W
        meta_ref[0, r] = start
        meta_ref[1, r] = owner
        hit = lane_owner == owner
        ids = jnp.where(hit & (lane_turn == turn), panel - owner * ADP_W, ids)
        return ids, jnp.where(hit, turn + 1, turn), start + length_ref[0, r]

    for table in tables:
        table.wait()
    nothing = jnp.zeros((1, 128), jnp.int32)
    ids_ref[...] = lax.fori_loop(0, count, route, (nothing, nothing, 0))[0]
    own_ids = pltpu.make_async_copy(ids_ref, ids_all.at[me], load_sem.at[4])
    own_ids.start()
    pl.semaphore_wait(barrier, steps + groups - 1)

    def ids_copy(i):
        return pltpu.make_async_remote_copy(
            ids_ref, ids_all.at[me], ids_send.at[i], ids_recv.at[i],
            device_id=(target(i), grp), device_id_type=MESH,
        )

    for i in range(steps):
        ids_copy(i).start()

    own_ids.wait()

    def ids_arrival(i):
        return pltpu.make_async_remote_copy(
            ids_ref, ids_all.at[source(i)], ids_send.at[i], ids_recv.at[i],
            device_id=(target(i), grp), device_id_type=MESH,
        )

    for i in range(steps):
        ids_arrival(i).wait()

    to_smem = pltpu.make_async_copy(ids_all, ids_smem, load_sem.at[5])
    to_smem.start()
    to_smem.wait()
    loads[0].wait()

    def down_copy(i):
        return pltpu.make_async_remote_copy(
            stage.at[i], held.at[i], down_send.at[i], down_recv.at[i],
            device_id=(target(i), grp), device_id_type=MESH,
        )

    def up_copy(i):
        return pltpu.make_async_remote_copy(
            stage_up.at[i], held_up.at[i], up_send.at[i], up_recv.at[i],
            device_id=(target(i), grp), device_id_type=MESH,
        )

    @pl.loop(0, steps)
    def _(i):
        to = target(i)
        stage[i, 0:64] = down[ids_smem[to, 0, 2 * me]]
        stage[i, 64:128] = down[ids_smem[to, 0, 2 * me + 1]]
        down_copy(i).start()

    held[steps, 0:64] = down[ids_smem[me, 0, 2 * me]]
    held[steps, 64:128] = down[ids_smem[me, 0, 2 * me + 1]]
    loads[1].wait()

    @pl.loop(0, steps)
    def _(i):
        to = target(i)
        stage_up[i, 0:64] = up[ids_smem[to, 0, 2 * me]]
        stage_up[i, 64:128] = up[ids_smem[to, 0, 2 * me + 1]]
        up_copy(i).start()

    held_up[steps, 0:64] = up[ids_smem[me, 0, 2 * me]]
    held_up[steps, 64:128] = up[ids_smem[me, 0, 2 * me + 1]]

    def base_copy(k, c):
        slot = 2 * k + c
        return pltpu.make_async_remote_copy(
            base_send.at[slot], base_held.at[2 * k + core], base_ssem.at[slot], base_rsem.at[2 * k + core],
            device_id=(me, ((my_x + k) % 4) * 2 + c), device_id_type=MESH,
        )

    def base_arrival(k, c):
        slot = 2 * k + c
        return pltpu.make_async_remote_copy(
            base_send.at[slot], base_held.at[slot], base_ssem.at[slot], base_rsem.at[slot],
            device_id=(me, ((my_x + k) % 4) * 2 + c), device_id_type=MESH,
        )

    loads[2].wait()
    loads[3].wait()

    @pl.loop(0, 4)
    def _(k):
        columns = pl.ds(pl.multiple_of(((my_x + k) % 4) * 256, 256), 256)

        @pl.loop(0, tokens_n // ROWS)
        def _(m):
            rows = pl.ds(pl.multiple_of(m * ROWS, ROWS), ROWS)
            part = jnp.dot(tokens[rows, :], weight[:, columns], preferred_element_type=F32)
            base_send[2 * k, rows] = part[:, :128]
            base_send[2 * k + 1, rows] = part[:, 128:]

        @pl.when(k == 0)
        def _():
            base_copy(0, 1 - core).start()

        @pl.when(k > 0)
        def _():
            base_copy(k, 0).start()
            base_copy(k, 1).start()

    lane = lax.broadcasted_iota(jnp.int32, (ROWS, 128), 1)
    row = lax.broadcasted_iota(jnp.int32, (ROWS, 128), 0)
    upper = jnp.where(lane < 64, 0, 1)

    @pl.loop(0, count)
    def _(r):
        def earlier(q, rank):
            return rank + jnp.where((meta_ref[1, q] == meta_ref[1, r]) & (q < r), 1, 0)

        meta_ref[2, r] = 2 * meta_ref[1, r] + lax.fori_loop(0, count, earlier, 0)

    @pl.loop(0, tokens_n // ROWS)
    def _(m):
        rows = pl.ds(pl.multiple_of(m * ROWS, ROWS), ROWS)
        at = row + m * ROWS
        slot = lax.fori_loop(
            0, count,
            lambda r, s: jnp.where(at >= meta_ref[0, r], meta_ref[2, r], s),
            jnp.zeros((ROWS, 128), jnp.int32),
        )
        code[rows] = slot - upper
        acc[rows] = jnp.zeros((ROWS, 128), F32)

    def shrink(j):
        down_copy(2 * j).wait_recv()

        @pl.when(2 * j + 1 < steps)
        def _():
            down_copy(2 * j + 1).wait_recv()

        first, second = 2 * source(2 * j), 2 * source(2 * j + 1)

        @pl.loop(0, tokens_n // 1024)
        def _(m):
            rows = pl.ds(pl.multiple_of(m * 1024, 1024), 1024)
            panels = held[pl.ds(2 * j, 2)].reshape(256, held.shape[2])
            part = lax.dot_general(
                tokens[rows, :], panels, (((1,), (1,)), ((), ())), preferred_element_type=F32
            )
            at = code[rows]
            acc[rows] += jnp.where(at == first, part[:, :128], 0.0) + jnp.where(at == second, part[:, 128:], 0.0)

    @pl.loop(0, owners // 2 - 4)
    def _(j):
        shrink(j)

    base_arrival(0, 1 - core).wait_recv()

    @pl.loop(1, 4)
    def _(k):
        base_arrival(k, 0).wait_recv()
        base_arrival(k, 1).wait_recv()

    @pl.loop(0, tokens_n // 256)
    def _(m):
        rows = pl.ds(pl.multiple_of(m * 256, 256), 256)
        total = base_send[core, rows] + base_held[1 - core, rows]
        for slot in range(2, 8):
            total = total + base_held[slot, rows]
        base_held[core, rows] = total

    @pl.loop(owners // 2 - 4, owners // 2)
    def _(j):
        shrink(j)

    half = lax.broadcasted_iota(jnp.int32, (128, 128), 1) < 64

    def pack(k):
        p = (grp + k) % groups
        top = acc[pl.ds(pl.multiple_of(p * 256, 256), 128)]
        low = acc[pl.ds(pl.multiple_of(p * 256 + 128, 128), 128)]
        packed[k] = jnp.where(half, top + pltpu.roll(top, 64, 1), low + pltpu.roll(low, 64, 1))

    def part_copy(k):
        return pltpu.make_async_remote_copy(
            packed.at[k], packed_held.at[k], part_ssem.at[k], part_rsem.at[k],
            device_id=(me, (grp + k) % groups), device_id_type=MESH,
        )

    @pl.loop(1, groups)
    def _(k):
        pack(k)
        part_copy(k).start()

    pack(0)

    @pl.loop(0, tokens_n // ROWS)
    def _(m):
        rows = pl.ds(pl.multiple_of(m * ROWS, ROWS), ROWS)
        acc[rows] = jnp.zeros((ROWS, 128), F32)

    total = packed[0]

    def add_part(k, s):
        part_copy(k).wait_recv()
        return s + packed_held[k]

    rounded[0] = lax.fori_loop(1, groups, add_part, total).astype(BF16)

    def full_copy(k):
        return pltpu.make_async_remote_copy(
            rounded.at[0], rounded.at[k], full_ssem.at[k], full_rsem.at[k],
            device_id=(me, (grp + k) % groups), device_id_type=MESH,
        )

    @pl.loop(1, groups)
    def _(k):
        full_copy(k).start()

    shrunk = base_send.at[1 - core]
    base_copy(0, 1 - core).wait_send()

    @pl.loop(1, 4)
    def _(k):
        base_copy(k, 0).wait_send()
        base_copy(k, 1).wait_send()

    def unpack(k):
        p = (grp + groups - k) % groups
        both = rounded[k].astype(F32)
        other = pltpu.roll(both, 64, 1)
        shrunk[pl.ds(pl.multiple_of(p * 256, 256), 128)] = jnp.where(half, both, other)
        shrunk[pl.ds(pl.multiple_of(p * 256 + 128, 128), 128)] = jnp.where(half, other, both)

    unpack(0)

    @pl.loop(1, groups)
    def _(k):
        full_copy(k).wait_recv()
        unpack(k)

    def arrive(first, count_up):
        @pl.loop(0, count_up)
        def _(a):
            @pl.when(first + a < steps)
            def _():
                up_copy(first + a).wait_recv()

    def term(first, count_up, rows):
        names = [2 * source(first + a) for a in range(count_up)]
        at, value = code[rows], shrunk[rows]
        spread = jnp.concatenate([jnp.where(at == n, value, 0.0).astype(BF16) for n in names], axis=1)
        panels = held_up[pl.ds(first, count_up)].reshape(count_up * 128, 128)
        return jnp.dot(spread, panels, preferred_element_type=F32)

    @pl.loop(0, owners // 8 - 1)
    def _(j):
        arrive(8 * j, 8)

        @pl.loop(0, tokens_n // ROWS)
        def _(m):
            rows = pl.ds(pl.multiple_of(m * ROWS, ROWS), ROWS)
            acc[rows] += term(8 * j, 8, rows)

    arrive(owners - 8, 8)

    @pl.loop(0, tokens_n // ROWS)
    def _(m):
        rows = pl.ds(pl.multiple_of(m * ROWS, ROWS), ROWS)
        delta = acc[rows] + term(owners - 8, 8, rows)
        out_ref[rows] = (base_held[core, rows] + delta.astype(BF16).astype(F32)).astype(BF16)

    @pl.loop(0, steps)
    def _(i):
        down_copy(i).wait_send()
        up_copy(i).wait_send()

    @pl.loop(1, groups)
    def _(k):
        part_copy(k).wait_send()
        full_copy(k).wait_send()


def settle(values_ref, out_ref):
    out_ref[...] = values_ref[...]


def shards(tokens, value_weight, down_panels, up_panels, request_adapter, request_length, adapter_panel_place):
    owners, groups = lax.axis_size("wide"), lax.axis_size("grp")
    rows, features = tokens.shape
    units = up_panels.shape[2]
    dma = pltpu.SemaphoreType.DMA
    vmem = pltpu.VMEM
    values = pl.pallas_call(
        functools.partial(kernel, owners, groups),
        out_shape=jax.ShapeDtypeStruct((rows, units), BF16),
        in_specs=[pl.BlockSpec(memory_space=pl.ANY)] * 7,
        out_specs=pl.BlockSpec(memory_space=pltpu.VMEM),
        scratch_shapes=[
            vmem(tokens.shape, BF16),
            vmem(value_weight.shape, BF16),
            vmem(down_panels.shape, BF16),
            vmem(up_panels.shape, BF16),
            vmem((owners - 1, 128, features), BF16),
            vmem((owners - 1, 128, units), BF16),
            vmem((owners, 128, features), BF16),
            vmem((owners, 128, units), BF16),
            vmem((groups, rows, units), F32),
            vmem((groups, rows, units), F32),
            vmem((rows, 128), F32),
            vmem((rows, 128), jnp.int32),
            vmem((groups, 128, 128), F32),
            vmem((groups, 128, 128), F32),
            vmem((groups, 128, 128), BF16),
            pltpu.SMEM(request_adapter.shape, jnp.int32),
            pltpu.SMEM(request_length.shape, jnp.int32),
            pltpu.SMEM(adapter_panel_place.shape, jnp.int32),
            vmem((1, 128), jnp.int32),
            vmem((owners, 1, 128), jnp.int32),
            pltpu.SMEM((owners, 1, 128), jnp.int32),
            pltpu.SMEM((3, request_adapter.shape[1]), jnp.int32),
            dma((9,)),
            dma((owners - 1,)),
            dma((owners - 1,)),
            dma((owners - 1,)),
            dma((owners - 1,)),
            dma((owners - 1,)),
            dma((owners - 1,)),
            dma((groups,)),
            dma((groups,)),
            dma((groups,)),
            dma((groups,)),
            dma((groups,)),
            dma((groups,)),
        ],
        compiler_params=pltpu.CompilerParams(
            collective_id=0, has_side_effects=True, vmem_limit_bytes=60 * 2**20
        ),
        name="routed_lora",
    )(request_adapter, request_length, adapter_panel_place, tokens, value_weight, down_panels, up_panels)
    return pl.pallas_call(
        settle,
        out_shape=jax.ShapeDtypeStruct((rows, units), BF16),
        in_specs=[pl.BlockSpec(memory_space=pltpu.VMEM)],
        out_specs=pl.BlockSpec(memory_space=pltpu.VMEM),
        name="settle",
    )(values)


def solution(mesh):
    placed = (
        P("wide", "grp"),
        P("grp", None),
        P("wide", None, "grp"),
        P("wide", None, "grp"),
        P("wide", None),
        P("wide", None),
        P(),
    )
    return jax.shard_map(
        shards, mesh=mesh, in_specs=placed, out_specs=P("wide", "grp"), check_vma=False
    )
```
